32 devices in a mesh: tm: 4 (over y, core), dom: 8 (over z, x).
Axes of the slice: x: 2, y: 2, z: 4, core: 2. Of those that a mesh axis runs over, the one named last changes fastest.
Arguments:
- particles: float32 [4, 64, 4096], P('tm', None, 'dom'), may hold values from -12 to 12, as said below
- noise: float32 [4, 64, 4096], P('tm', None, 'dom'), may hold values from -6 to 6
Outputs:
- advanced: float32 [4, 64, 4096], P('tm', None, 'dom')
The draws below stay inside these ranges and needn't reach their ends.
Inputs may be any that keep to these rules, and one draw needn't show every extreme that they name: `particles`: positions of cells in principal components, each time point about a shifted centre.
All inputs are finite; a program needn't handle non-finite values.
Results may differ from the reference program's by a relative error of at most 0.012.
The reference program's roundings to bfloat16 on the way count: a program that leaves them out, or rounds other values in their place, can miss the bound.
Values may be sent and summed in bfloat16 or wider, within the bound.
A program may use at most 64 MiB of HBM per device.

```python
import math
import jax
import jax.numpy as jnp
from jax import lax

DIM = 64
SWEEPS = 2
NPART = 4096
TIMES = 4


def draw_particles(key, part):
    shape = (TIMES, DIM, NPART)
    centres = 0.3 * jnp.arange(TIMES, dtype=jnp.float32)[:, None, None]
    base = jnp.clip(jax.random.normal(jax.random.fold_in(key, 3), shape, jnp.float32), -6.0, 6.0)
    return base + centres


def block_levels(rng, shape, cuts, smallest, high):
    gain, own = 1.0, jax.random.fold_in(rng, 6)
    for axis_at, blocks in cuts:
        heights = jnp.exp(jax.random.uniform(jax.random.fold_in(own, axis_at), (blocks,), jnp.float32, smallest / len(cuts), high / len(cuts)))
        gain = gain * jnp.repeat(heights, shape[axis_at] // blocks).reshape([-1 if axis == axis_at else 1 for axis in range(len(shape))])
    return gain


def centred(own_key, shape, deviation, reach, shards=(), kind=jnp.bfloat16):
    loudness = block_levels(own_key, shape, shards, -0.22, 0.18) if shards else 1.0
    values = jax.random.normal(own_key, shape, jnp.float32) * deviation * loudness
    return jnp.minimum(jnp.maximum(values, -reach), reach).astype(kind)


def setup_inputs(seed: int = 0) -> dict:
    arg_keys = jax.random.split(jax.random.key(seed), 3)
    particles = draw_particles(jax.random.fold_in(arg_keys[2], 71), 0)
    noise = centred(arg_keys[1], (TIMES, DIM, NPART), 1.0, 6.0, ((0, 4), (2, 8)), jnp.float32)
    return {"particles": particles, "noise": noise}


EPS = 4.0
STEP = 0.5
TEMP = 0.05

def row_blocks(sources):
    row_count = sources.shape[1]
    row_width = math.gcd(row_count, 512)
    return sources.reshape(DIM, row_count // row_width, row_width).transpose(1, 0, 2)

def scores_of(sources, targets, potential):
    products = lax.dot_general(sources, targets, (((0,), (0,)), ((), ())), preferred_element_type=jnp.float32)
    return (products + potential[None, :]) / EPS

def update(sources, targets, potential):
    col_count = targets.shape[1]

    def per_block(blocks):
        scores = scores_of(blocks, targets, potential)
        highest = lax.optimization_barrier(jnp.max(scores, axis=1, keepdims=True))
        totals = lax.optimization_barrier(jnp.sum(jnp.exp(scores - highest), axis=1))
        return -EPS * (highest[:, 0] + jnp.log(totals)) + EPS * math.log(col_count)
    return lax.map(per_block, row_blocks(sources)).reshape(sources.shape[1])

def barycentre(sources, targets, potential):

    def per_block(blocks):
        scores = scores_of(blocks, targets, potential)
        highest = lax.optimization_barrier(jnp.max(scores, axis=1, keepdims=True))
        shifted = jnp.exp(scores - highest)
        totals = lax.optimization_barrier(jnp.sum(shifted, axis=1, keepdims=True))
        weights = (shifted / totals).astype(jnp.bfloat16)
        return lax.dot_general(targets, weights, (((1,), (1,)), ((), ())), preferred_element_type=jnp.float32)
    result = lax.map(per_block, row_blocks(sources))
    return result.transpose(1, 0, 2).reshape(DIM, sources.shape[1])

def reference(particles, noise):
    rounded = particles.astype(jnp.bfloat16)
    half_square = 0.5 * lax.optimization_barrier(jnp.sum(jnp.square(rounded.astype(jnp.float32)), axis=1))
    source_pot = [None] * (TIMES - 1)
    target_pot = [-half_square[moment + 1] for moment in range(TIMES - 1)]
    for sweep_index in range(SWEEPS):
        for moment in range(TIMES - 1):
            source_pot[moment] = update(rounded[moment], rounded[moment + 1], target_pot[moment])
            target_pot[moment] = update(rounded[moment + 1], rounded[moment], source_pot[moment])
    results = []
    for moment in range(TIMES):
        pull = jnp.zeros((DIM, NPART), jnp.float32)
        if moment < TIMES - 1:
            pull = pull + (particles[moment] - barycentre(rounded[moment], rounded[moment + 1], target_pot[moment]))
        if moment > 0:
            pull = pull + (particles[moment] - barycentre(rounded[moment], rounded[moment - 1], source_pot[moment - 1]))
        results.append(particles[moment] - STEP * pull + math.sqrt(2.0 * STEP * TEMP) * noise[moment])
    return jnp.stack(results)
```

```python
import functools
import math

import jax
import jax.numpy as jnp
from jax import lax
from jax.experimental import pallas as pl
from jax.experimental.pallas import tpu as pltpu
from jax.sharding import PartitionSpec as P

SWEEPS = 2
EPS = 4.0
STEP = 0.5
TEMP = 0.05
MESH = pl.DeviceIdType.MESH
EXTRA = 16
PIECE = 64
CHUNK = 512
LAG = 4
TILE = 128
LANES = 128


def crossed(me, i, n):
    total = 0
    bit = 1
    while bit < n:
        mine, its = (me // bit) % 2, (i // bit) % 2
        total = total + bit * (mine + its - 2 * mine * its)
        bit *= 2
    return total


def split3(value):
    high = value.astype(jnp.bfloat16).astype(jnp.float32)
    rest = value - high
    middle = rest.astype(jnp.bfloat16).astype(jnp.float32)
    return high, middle, rest - middle


def dot(a, b, dims):
    return lax.dot_general(a, b, (dims, ((), ())), preferred_element_type=jnp.float32)


def kernel(
    times, n, points_ref, noise_ref, out_ref,
    own, nxt, prv, lall, lown, ppot, spot, xa, xt, ya, yb, yx, y2, kept, gam, csum, pair, sa, sb, pw, m_ref, l_ref, acc, wide,
    own_s, own_r, nxt_s, nxt_r, prv_s, prv_r, lall_s, lall_r, ppot_s, ppot_r,
):
    t = lax.axis_index("tm")
    me = lax.axis_index("dom")
    dim, width = points_ref.shape
    has_next = t < times - 1
    has_prev = t > 0
    low = 2 if n > 1 else 1
    half = max(n // 2, 1)

    points = points_ref[...]
    rounded = points.astype(jnp.bfloat16)
    own[me] = rounded
    xa[pl.ds(0, dim), :] = (rounded.astype(jnp.float32) * (1.0 / EPS)).astype(jnp.bfloat16)
    rows = lax.broadcasted_iota(jnp.int32, (EXTRA, width), 0)
    xa[pl.ds(dim, EXTRA), :] = jnp.where(rows < 3, 1.0 / EPS, 0.0).astype(jnp.bfloat16)

    barrier = pltpu.get_barrier_semaphore()
    same = [i for i in range(1, n) if i % low == 0 or i == 1]
    for i in same:
        pl.semaphore_signal(barrier, inc=1, device_id=(t, crossed(me, i, n)), device_id_type=MESH)

    @pl.when(has_next)
    def _():
        pl.semaphore_signal(barrier, inc=1, device_id=(t + 1, me), device_id_type=MESH)

    @pl.when(has_prev)
    def _():
        pl.semaphore_signal(barrier, inc=1, device_id=(t - 1, me), device_id_type=MESH)

    sides = has_next.astype(jnp.int32) + has_prev.astype(jnp.int32)
    pl.semaphore_wait(barrier, len(same) + sides)

    def own_copy(i, block, slot):
        return pltpu.make_async_remote_copy(
            src_ref=own.at[block], dst_ref=own.at[block], send_sem=own_s.at[slot], recv_sem=own_r.at[block],
            device_id=(t, crossed(me, i, n)), device_id_type=MESH)

    def to_prev(block):
        return pltpu.make_async_remote_copy(
            src_ref=own.at[block], dst_ref=nxt.at[block], send_sem=nxt_s.at[block], recv_sem=nxt_r.at[block],
            device_id=(t - 1, me), device_id_type=MESH)

    def to_next(block):
        return pltpu.make_async_remote_copy(
            src_ref=own.at[block], dst_ref=prv.at[block], send_sem=prv_s.at[block], recv_sem=prv_r.at[block],
            device_id=(t + 1, me), device_id_type=MESH)

    for i in range(low, n, low):
        own_copy(i, me, i).start()

    def pass_on(i):
        block = crossed(me, i, n)
        if i > 0:
            own_copy(i if i % low == 0 else 1, block, 0).wait_recv()
        if i % low == 0 and low > 1:
            own_copy(1, block, i + 1).start()

        @pl.when(has_prev)
        def _():
            to_prev(block).start()

        @pl.when(has_next)
        def _():
            to_next(block).start()

    order = [0]
    for i in range(low, n, low):
        order += [i, i - low + 1] if low > 1 else [i]
    if low > 1:
        order.append(n - 1)
    def extend(y_ref, block_ref, pot, ones):
        y_ref[pl.ds(0, dim), :] = block_ref[...]
        high, middle, least = split3(pot)
        tail = jnp.where((rows >= 3) & (rows < 6), ones, 0.0)
        pieces = jnp.where(rows == 0, high, jnp.where(rows == 1, middle, jnp.where(rows == 2, least, tail)))
        y_ref[pl.ds(dim, EXTRA), :] = pieces.astype(jnp.bfloat16)

    def folded(values, join):
        parts = [values[r:r + 8] for r in range(0, values.shape[0], 8)]
        while len(parts) > 1:
            parts = [join(parts[k], parts[k + 1]) for k in range(0, len(parts) - 1, 2)] + (
                [parts[-1]] if len(parts) % 2 else [])
        return parts[0]

    def reset():
        m_ref[...] = jnp.full_like(m_ref, -jnp.inf)
        l_ref[...] = jnp.zeros_like(l_ref)

    def step(y_ref, new_scores, old_scores, old_block, mean):
        m_old = m_ref[...]
        highest, total = None, None
        if old_scores is not None:
            for start in range(0, width, PIECE):
                here = pl.ds(start, PIECE)
                weights = jnp.exp(old_scores[here, :] - m_old)
                part = folded(weights, jnp.add)
                total = part if total is None else total + part
                if mean:
                    pw[here, :] = weights.astype(jnp.bfloat16)
        if new_scores is not None:
            for start in range(0, width, CHUNK):
                here = pl.ds(start, CHUNK)
                scores = lax.dot_general(
                    y_ref[:, here], xa[...], (((0,), (0,)), ((), ())), preferred_element_type=jnp.float32)
                new_scores[here, :] = scores
                top = folded(scores, jnp.maximum)
                highest = top if highest is None else jnp.maximum(highest, top)
        if old_scores is not None:
            sums = l_ref[...] + jnp.sum(total, axis=0, keepdims=True)
            if mean:
                for start in range(0, width, CHUNK):
                    here = pl.ds(start, CHUNK)
                    acc[...] += lax.dot_general(
                        old_block[:, here], pw[here, :], (((1,), (0,)), ((), ())),
                        preferred_element_type=jnp.float32)
        else:
            sums = l_ref[...]
        if new_scores is not None:
            m_new = jnp.maximum(m_old, jnp.max(highest, axis=0, keepdims=True))
            scale = jnp.exp(m_old - m_new)
            m_ref[...] = m_new
            sums = sums * scale
            if mean and old_scores is not None:
                acc[...] = acc[...] * scale
        l_ref[...] = sums

    def sweep_over(prepare, slots, mean):
        def do(i, y_ref, new, old):
            prepare(y_ref, i)
            step(y_ref, new, old, slots.at[crossed(me, i - 1, n)], mean)

        prepare(ya, 0)
        step(ya, sa, None, None, mean)
        if n > 2:
            @pl.loop(0, n // 2 - 1)
            def _(h):
                do(2 * h + 1, yb, sb, sa)
                do(2 * h + 2, ya, sa, sb)
        do(n - 1, yb, sb, sa)
        step(None, None, sb, slots.at[crossed(me, n - 1, n)], mean)

    def spot_copy(i):
        return pltpu.make_async_remote_copy(
            src_ref=spot, dst_ref=ppot.at[me], send_sem=ppot_s.at[i],
            recv_sem=ppot_r.at[me], device_id=(t + 1, crossed(me, i, n)), device_id_type=MESH)

    def await_ppot(block):
        pltpu.make_async_remote_copy(
            src_ref=spot, dst_ref=ppot.at[block], send_sem=ppot_s.at[0],
            recv_sem=ppot_r.at[block], device_id=(t - 1, block), device_id_type=MESH).wait_recv()

    def sum_copy(sweep, part, i, block):
        some = pl.ds(part * half, half)
        return pltpu.make_async_remote_copy(
            src_ref=lown.at[sweep, some], dst_ref=lall.at[sweep, block, some], send_sem=lall_s.at[sweep, part, i],
            recv_sem=lall_r.at[sweep, part, block], device_id=(t, crossed(me, i, n)), device_id_type=MESH)

    def send_sums(sweep, part):
        some = pl.ds(part * half, half)
        lown[sweep, some] = gam[some] + jnp.log(csum[some])
        for i in reversed(range(1, n)):
            sum_copy(sweep, part, i, me).start()

    def factors(sweep):
        for i in range(1, n):
            for part in range(n // half):
                sum_copy(sweep, part, 0, crossed(me, i, n)).wait_recv()
        lall[sweep, me] = lown[sweep]
        top = lall[sweep, 0]
        for k in range(1, n):
            top = jnp.maximum(top, lall[sweep, k])
        total = jnp.exp(lall[sweep, 0] - top)
        for k in range(1, n):
            total = total + jnp.exp(lall[sweep, k] - top)
        return jnp.exp(gam[...] - (top + jnp.log(total)))

    def landed(block, slots, sends, recvs):
        pltpu.make_async_remote_copy(
            src_ref=own.at[block], dst_ref=slots.at[block], send_sem=sends.at[block], recv_sem=recvs.at[block],
            device_id=(t, me), device_id_type=MESH).wait_recv()

    def first_prepare(y_ref, i):
        block = crossed(me, i, n)
        landed(block, nxt, nxt_s, nxt_r)
        extend(y_ref, nxt.at[block], -0.5 * jnp.sum(
            jnp.square(nxt[block].astype(jnp.float32)), axis=0, keepdims=True), 1.0)

    @pl.when(has_next)
    def _():
        reset()

    def first_step(k):
        @pl.when(has_next)
        def _():
            new, old = (sa, sb) if k % 2 == 0 else (sb, sa)
            y_ref = yx.at[crossed(me, order[k], n)]
            first_prepare(y_ref, order[k])
            step(y_ref, new, old if k > 0 else None, None, False)

    for k in range(n):
        pass_on(order[k])
        if k >= LAG:
            first_step(k - LAG)
    for k in range(max(0, n - LAG), n):
        first_step(k)

    @pl.when(has_next)
    def _():
        step(None, None, sb if n % 2 == 0 else sa, None, False)
        shift = -(m_ref[...] + jnp.log(l_ref[...]))
        m_ref[...] = shift
        high, middle, least = split3(shift)
        xa[pl.ds(dim, EXTRA), :] = jnp.where(rows < 3, 1.0 / EPS, jnp.where(rows == 3, high, jnp.where(
            rows == 4, middle, jnp.where(rows == 5, least, 0.0)))).astype(jnp.bfloat16)
        xt[...] = xa[...].astype(jnp.float32).T.astype(jnp.bfloat16)

        for b in range(n):
            new = sa if b % 2 == 0 else sb
            cols = pl.ds(b * width, width)
            top = None
            for start in range(0, width, TILE):
                here = pl.ds(start, TILE)
                scores = dot(xt[here, :], yx[b], ((1,), (0,)))
                new[here, :] = scores
                part = folded(scores, jnp.maximum)
                top = part if top is None else jnp.maximum(top, part)
            top = jnp.max(top, axis=0, keepdims=True)
            total = None
            for start in range(0, width, TILE):
                here = pl.ds(start, TILE)
                weights = jnp.exp(new[here, :] - top)
                kept[here, cols] = weights.astype(jnp.bfloat16)
                part = folded(weights, jnp.add)
                total = part if total is None else total + part
            gam[pl.ds(b, 1), :] = top
            csum[pl.ds(b, 1), :] = jnp.sum(total, axis=0, keepdims=True)
            if (b + 1) % half == 0:
                send_sums(0, b // half)

        scale = factors(0)
        high = scale.astype(jnp.bfloat16)
        pair[pl.ds(0, n), :] = high.astype(jnp.float32)
        pair[pl.ds(n, n), :] = scale - high.astype(jnp.float32)
        both = pair[...].astype(jnp.bfloat16)
        row = lax.broadcasted_iota(jnp.int32, (2 * n, width), 0)
        total = jnp.zeros((2 * n, width), jnp.float32)
        for b in range(n):
            part = dot(both, kept[:, pl.ds(b * width, width)], ((1,), (1,)))
            total = total + jnp.where((row == b) | (row == n + b), part, 0.0)
        total = jnp.sum(total, axis=0, keepdims=True)
        spot[...] = EPS * (m_ref[...] - jnp.log(total))
        for i in reversed(range(n)):
            spot_copy(i).start()
        ratio = 1.0 / total
        high = ratio.astype(jnp.bfloat16).astype(jnp.float32)
        both = jnp.where(rows == 0, high, jnp.where(rows == 1, ratio - high, 0.0)).astype(jnp.bfloat16)
        for b in range(n):
            part = dot(both, kept[:, pl.ds(b * width, width)], ((1,), (0,)))
            csum[pl.ds(b, 1), :] = jnp.sum(part, axis=0, keepdims=True)
            if (b + 1) % half == 0:
                send_sums(1, b // half)

    @pl.when(has_prev)
    def _():
        def prepare(y_ref, i):
            block = crossed(me, i, n)
            landed(block, prv, prv_s, prv_r)
            await_ppot(block)
            extend(y_ref, prv.at[block], ppot[block], 0.0)

        reset()
        acc[...] = jnp.zeros_like(acc)
        sweep_over(prepare, prv, True)
        out_ref[...] = points_ref[...] - STEP * (points_ref[...] - acc[...] / l_ref[...]) + (
            math.sqrt(2.0 * STEP * TEMP) * noise_ref[...])

    @pl.when(jnp.logical_not(has_prev))
    def _():
        out_ref[...] = points_ref[...] + math.sqrt(2.0 * STEP * TEMP) * noise_ref[...]

    @pl.when(has_next)
    def _():
        gam[...] = factors(1)
        side = dim + EXTRA
        lane = wide.shape[1] // 2
        y2[...] = jnp.zeros_like(y2)
        for b in range(n):
            scaled = yx[b].astype(jnp.float32) * gam[pl.ds(b, 1), :]
            high = scaled.astype(jnp.bfloat16)
            y2[b % 2, pl.ds(0, side), :] = high
            y2[b % 2, pl.ds(lane, side), :] = (scaled - high.astype(jnp.float32)).astype(jnp.bfloat16)
            part = dot(kept[:, pl.ds(b * width, width)], y2[b % 2], ((1,), (1,)))
            wide[...] = part if b == 0 else wide[...] + part
        mean = (wide[:, pl.ds(0, lane)] + wide[:, pl.ds(lane, lane)]).T
        out_ref[...] = out_ref[...] - STEP * (points_ref[...] - mean[:dim] / mean[dim + 3:dim + 4])

    for i in range(low, n, low):
        own_copy(i, me, i).wait_send()
    if low > 1:
        for i in range(0, n, low):
            own_copy(1, crossed(me, i, n), i + 1).wait_send()

    @pl.when(has_prev)
    def _():
        for i in range(n):
            to_prev(i).wait_send()

    @pl.when(has_next)
    def _():
        for i in range(n):
            to_next(i).wait_send()
            spot_copy(i).wait_send()
        for sweep in range(SWEEPS):
            for part in range(n // half):
                for i in range(1, n):
                    sum_copy(sweep, part, i, me).wait_send()


def per_device(times, n, particles, noise):
    points = particles[0]
    dim, width = points.shape
    dma = pltpu.SemaphoreType.DMA
    row = (1, width)
    tall = dim + EXTRA
    lanes = -(-tall // LANES) * LANES
    advanced = pl.pallas_call(
        functools.partial(kernel, times, n),
        out_shape=jax.ShapeDtypeStruct((dim, width), jnp.float32),
        in_specs=[pl.BlockSpec(memory_space=pltpu.VMEM)] * 2,
        out_specs=pl.BlockSpec(memory_space=pltpu.VMEM),
        scratch_shapes=[
            pltpu.VMEM((n, dim, width), jnp.bfloat16),
            pltpu.VMEM((n, dim, width), jnp.bfloat16),
            pltpu.VMEM((n, dim, width), jnp.bfloat16),
            pltpu.VMEM((SWEEPS, n, n, width), jnp.float32),
            pltpu.VMEM((SWEEPS, n, width), jnp.float32),
            pltpu.VMEM((n,) + row, jnp.float32),
            pltpu.VMEM(row, jnp.float32),
            pltpu.VMEM((tall, width), jnp.bfloat16),
            pltpu.VMEM((width, tall), jnp.bfloat16),
            pltpu.VMEM((tall, width), jnp.bfloat16),
            pltpu.VMEM((tall, width), jnp.bfloat16),
            pltpu.VMEM((n, tall, width), jnp.bfloat16),
            pltpu.VMEM((2, 2 * lanes, width), jnp.bfloat16),
            pltpu.VMEM((width, n * width), jnp.bfloat16),
            pltpu.VMEM((n, width), jnp.float32),
            pltpu.VMEM((n, width), jnp.float32),
            pltpu.VMEM((2 * n, width), jnp.float32),
            pltpu.VMEM((width, width), jnp.float32),
            pltpu.VMEM((width, width), jnp.float32),
            pltpu.VMEM((width, width), jnp.bfloat16),
            pltpu.VMEM(row, jnp.float32),
            pltpu.VMEM(row, jnp.float32),
            pltpu.VMEM((dim, width), jnp.float32),
            pltpu.VMEM((width, 2 * lanes), jnp.float32),
            dma((n,)), dma((n,)), dma((n,)), dma((n,)), dma((n,)), dma((n,)),
            dma((SWEEPS, 2, n)), dma((SWEEPS, 2, n)), dma((n,)), dma((n,)),
        ],
        compiler_params=pltpu.CompilerParams(collective_id=0, has_side_effects=True),
    )(points, noise[0])
    return advanced[None]


def solution(mesh):
    times, n = mesh.shape["tm"], mesh.shape["dom"]
    assert n & (n - 1) == 0
    spec = P("tm", None, "dom")
    return jax.shard_map(
        functools.partial(per_device, times, n), mesh=mesh, in_specs=(spec, spec), out_specs=spec, check_vma=False)
```

```python
import functools
import math

import jax
import jax.numpy as jnp
from jax import lax
from jax.experimental import pallas as pl
from jax.experimental.pallas import tpu as pltpu
from jax.sharding import PartitionSpec as P

SWEEPS = 2
EPS = 4.0
STEP = 0.5
TEMP = 0.05
MESH = pl.DeviceIdType.MESH
EXTRA = 16
PIECE = 64
CHUNK = 512
LAG = 1
TILE = 128
LANES = 128


def crossed(me, i, n):
    total = 0
    bit = 1
    while bit < n:
        mine, its = (me // bit) % 2, (i // bit) % 2
        total = total + bit * (mine + its - 2 * mine * its)
        bit *= 2
    return total


def split3(value):
    high = value.astype(jnp.bfloat16).astype(jnp.float32)
    rest = value - high
    middle = rest.astype(jnp.bfloat16).astype(jnp.float32)
    return high, middle, rest - middle


def dot(a, b, dims):
    return lax.dot_general(a, b, (dims, ((), ())), preferred_element_type=jnp.float32)


def kernel(
    times, n, points_ref, noise_ref, out_ref,
    points, noise, own, nxt, prv, lall, lown, ppot, spot, xa, xt, ya, yb, yx, y2, kept, gam, csum, pair, sa, sb, pw,
    m_ref, l_ref, acc, wide, load, nxt_s, nxt_r, prv_s, prv_r, row_s, side_s, near_s, lall_s, lall_r, ppot_s, ppot_r,
):
    t = lax.axis_index("tm")
    me = lax.axis_index("dom")
    dim, width = points.shape
    has_next = t < times - 1
    has_prev = t > 0
    low = 2 if n > 1 else 1
    half = max(n // 2, 1)

    loads = [pltpu.make_async_copy(points_ref, points, load.at[0]), pltpu.make_async_copy(noise_ref, noise, load.at[1])]
    for copy in loads:
        copy.start()
    row_ids = range(0, n, low)
    barrier = pltpu.get_barrier_semaphore()

    def greet(*device):
        pl.semaphore_signal(barrier, inc=1, device_id=device, device_id_type=MESH)

    if low > 1:
        greet(t, crossed(me, 1, n))

    @pl.when(has_next)
    def _():
        for i in row_ids:
            greet(t + 1, crossed(me, i, n))

    @pl.when(t >= 2)
    def _():
        greet(t - 2, me)

    @pl.when(t == 1)
    def _():
        for i in row_ids:
            greet(0, crossed(me, i, n))

    loads[0].wait()
    rounded = points[...].astype(jnp.bfloat16)
    own[...] = rounded
    xa[pl.ds(0, dim), :] = (rounded.astype(jnp.float32) * (1.0 / EPS)).astype(jnp.bfloat16)
    rows = lax.broadcasted_iota(jnp.int32, (EXTRA, width), 0)
    xa[pl.ds(dim, EXTRA), :] = jnp.where(rows < 3, 1.0 / EPS, 0.0).astype(jnp.bfloat16)

    pl.semaphore_wait(barrier, low - 1 + len(row_ids) + (t < times - 2).astype(jnp.int32))

    def to_row(slots, sends, recvs, i, step):
        return pltpu.make_async_remote_copy(
            src_ref=own, dst_ref=slots.at[me], send_sem=sends.at[i], recv_sem=recvs.at[me],
            device_id=(t + step, crossed(me, i, n)), device_id_type=MESH)

    def to_side(slots, sends, recvs, block):
        return pltpu.make_async_remote_copy(
            src_ref=slots.at[block], dst_ref=slots.at[block], send_sem=sends.at[block], recv_sem=recvs.at[block],
            device_id=(t, crossed(me, 1, n)), device_id_type=MESH)

    def to_after(block):
        return pltpu.make_async_remote_copy(
            src_ref=nxt.at[block], dst_ref=prv.at[block], send_sem=prv_s.at[block], recv_sem=prv_r.at[block],
            device_id=(t + 2, me), device_id_type=MESH)

    row_order = [0] + list(reversed(row_ids[1:]))
    order = row_order + [i + 1 for i in row_order if low > 1]

    @pl.when(has_prev)
    def _():
        for i in row_order:
            to_row(nxt, nxt_s, nxt_r, i, -1).start()

    def pass_on(k):
        i = order[k]
        block = crossed(me, i, n)

        @pl.when(has_next)
        def _():
            landed(block, nxt, nxt_s, nxt_r)
            if i % low == 0 and low > 1:
                to_side(nxt, side_s, nxt_r, block).start()

        @pl.when(t < times - 2)
        def _():
            to_after(block).start()

        if k == len(row_order) - 1:
            @pl.when(t == 0)
            def _():
                for i in row_order:
                    to_row(prv, row_s, prv_r, i, 1).start()

    def extend(y_ref, block_ref, pot, ones):
        y_ref[pl.ds(0, dim), :] = block_ref[...]
        high, middle, least = split3(pot)
        tail = jnp.where((rows >= 3) & (rows < 6), ones, 0.0)
        pieces = jnp.where(rows == 0, high, jnp.where(rows == 1, middle, jnp.where(rows == 2, least, tail)))
        y_ref[pl.ds(dim, EXTRA), :] = pieces.astype(jnp.bfloat16)

    def folded(values, join):
        parts = [values[r:r + 8] for r in range(0, values.shape[0], 8)]
        while len(parts) > 1:
            parts = [join(parts[k], parts[k + 1]) for k in range(0, len(parts) - 1, 2)] + (
                [parts[-1]] if len(parts) % 2 else [])
        return parts[0]

    def reset():
        m_ref[...] = jnp.full_like(m_ref, -jnp.inf)
        l_ref[...] = jnp.zeros_like(l_ref)

    def step(y_ref, new_scores, old_scores, old_block, mean):
        m_old = m_ref[...]
        highest, total = None, None
        if old_scores is not None:
            for start in range(0, width, PIECE):
                here = pl.ds(start, PIECE)
                weights = jnp.exp(old_scores[here, :] - m_old)
                part = folded(weights, jnp.add)
                total = part if total is None else total + part
                if mean:
                    pw[here, :] = weights.astype(jnp.bfloat16)
        if new_scores is not None:
            for start in range(0, width, CHUNK):
                here = pl.ds(start, CHUNK)
                scores = lax.dot_general(
                    y_ref[:, here], xa[...], (((0,), (0,)), ((), ())), preferred_element_type=jnp.float32)
                new_scores[here, :] = scores
                top = folded(scores, jnp.maximum)
                highest = top if highest is None else jnp.maximum(highest, top)
        if old_scores is not None:
            sums = l_ref[...] + jnp.sum(total, axis=0, keepdims=True)
            if mean:
                for start in range(0, width, CHUNK):
                    here = pl.ds(start, CHUNK)
                    acc[...] += lax.dot_general(
                        old_block[:, here], pw[here, :], (((1,), (0,)), ((), ())),
                        preferred_element_type=jnp.float32)
        else:
            sums = l_ref[...]
        if new_scores is not None:
            m_new = jnp.maximum(m_old, jnp.max(highest, axis=0, keepdims=True))
            scale = jnp.exp(m_old - m_new)
            m_ref[...] = m_new
            sums = sums * scale
            if mean and old_scores is not None:
                acc[...] = acc[...] * scale
        l_ref[...] = sums

    def sweep_over(prepare, slots, mean):
        def do(i, y_ref, new, old):
            prepare(y_ref, i)
            step(y_ref, new, old, slots.at[crossed(me, i - 1, n)], mean)

        prepare(ya, 0)
        step(ya, sa, None, None, mean)
        if n > 2:
            @pl.loop(0, n // 2 - 1)
            def _(h):
                do(2 * h + 1, yb, sb, sa)
                do(2 * h + 2, ya, sa, sb)
        do(n - 1, yb, sb, sa)
        step(None, None, sb, slots.at[crossed(me, n - 1, n)], mean)

    def spot_copy(i):
        return pltpu.make_async_remote_copy(
            src_ref=spot, dst_ref=ppot.at[me], send_sem=ppot_s.at[i],
            recv_sem=ppot_r.at[me], device_id=(t + 1, crossed(me, i, n)), device_id_type=MESH)

    def await_ppot(block):
        pltpu.make_async_remote_copy(
            src_ref=spot, dst_ref=ppot.at[block], send_sem=ppot_s.at[0],
            recv_sem=ppot_r.at[block], device_id=(t - 1, block), device_id_type=MESH).wait_recv()

    def sum_copy(sweep, part, i, block):
        some = pl.ds(part * half, half)
        return pltpu.make_async_remote_copy(
            src_ref=lown.at[sweep, some], dst_ref=lall.at[sweep, block, some], send_sem=lall_s.at[sweep, part, i],
            recv_sem=lall_r.at[sweep, part, block], device_id=(t, crossed(me, i, n)), device_id_type=MESH)

    def send_sums(sweep, part):
        some = pl.ds(part * half, half)
        lown[sweep, some] = gam[some] + jnp.log(csum[some])
        for i in reversed(range(1, n)):
            sum_copy(sweep, part, i, me).start()

    def factors(sweep):
        for i in range(1, n):
            for part in range(n // half):
                sum_copy(sweep, part, 0, crossed(me, i, n)).wait_recv()
        lall[sweep, me] = lown[sweep]
        top = lall[sweep, 0]
        for k in range(1, n):
            top = jnp.maximum(top, lall[sweep, k])
        total = jnp.exp(lall[sweep, 0] - top)
        for k in range(1, n):
            total = total + jnp.exp(lall[sweep, k] - top)
        return jnp.exp(gam[...] - (top + jnp.log(total)))

    def landed(block, slots, sends, recvs):
        pltpu.make_async_remote_copy(
            src_ref=slots.at[block], dst_ref=slots.at[block], send_sem=sends.at[block], recv_sem=recvs.at[block],
            device_id=(t, me), device_id_type=MESH).wait_recv()

    def first_prepare(y_ref, i):
        block = crossed(me, i, n)
        extend(y_ref, nxt.at[block], -0.5 * jnp.sum(
            jnp.square(nxt[block].astype(jnp.float32)), axis=0, keepdims=True), 1.0)

    @pl.when(has_next)
    def _():
        reset()

    def first_step(k):
        @pl.when(has_next)
        def _():
            new, old = (sa, sb) if k % 2 == 0 else (sb, sa)
            y_ref = yx.at[crossed(me, order[k], n)]
            first_prepare(y_ref, order[k])
            step(y_ref, new, old if k > 0 else None, None, False)

    for k in range(n):
        pass_on(k)
        if k >= LAG:
            first_step(k - LAG)
    for k in range(max(0, n - LAG), n):
        first_step(k)

    @pl.when(has_next)
    def _():
        step(None, None, sb if n % 2 == 0 else sa, None, False)
        shift = -(m_ref[...] + jnp.log(l_ref[...]))
        m_ref[...] = shift
        high, middle, least = split3(shift)
        xa[pl.ds(dim, EXTRA), :] = jnp.where(rows < 3, 1.0 / EPS, jnp.where(rows == 3, high, jnp.where(
            rows == 4, middle, jnp.where(rows == 5, least, 0.0)))).astype(jnp.bfloat16)
        xt[...] = xa[...].astype(jnp.float32).T.astype(jnp.bfloat16)

        for b in range(n):
            new = sa if b % 2 == 0 else sb
            cols = pl.ds(b * width, width)
            top = None
            for start in range(0, width, TILE):
                here = pl.ds(start, TILE)
                scores = dot(xt[here, :], yx[b], ((1,), (0,)))
                new[here, :] = scores
                part = folded(scores, jnp.maximum)
                top = part if top is None else jnp.maximum(top, part)
            top = jnp.max(top, axis=0, keepdims=True)
            total = None
            for start in range(0, width, TILE):
                here = pl.ds(start, TILE)
                weights = jnp.exp(new[here, :] - top)
                kept[here, cols] = weights.astype(jnp.bfloat16)
                part = folded(weights, jnp.add)
                total = part if total is None else total + part
            gam[pl.ds(b, 1), :] = top
            csum[pl.ds(b, 1), :] = jnp.sum(total, axis=0, keepdims=True)
            if (b + 1) % half == 0:
                send_sums(0, b // half)

        if low > 1:
            @pl.when(t == 1)
            def _():
                for i in row_order:
                    block = crossed(me, i, n)
                    landed(block, prv, prv_s, prv_r)
                    to_side(prv, near_s, prv_r, block).start()

        scale = factors(0)
        high = scale.astype(jnp.bfloat16)
        pair[pl.ds(0, n), :] = high.astype(jnp.float32)
        pair[pl.ds(n, n), :] = scale - high.astype(jnp.float32)
        both = pair[...].astype(jnp.bfloat16)
        row = lax.broadcasted_iota(jnp.int32, (2 * n, width), 0)
        total = jnp.zeros((2 * n, width), jnp.float32)
        for b in range(n):
            part = dot(both, kept[:, pl.ds(b * width, width)], ((1,), (1,)))
            total = total + jnp.where((row == b) | (row == n + b), part, 0.0)
        total = jnp.sum(total, axis=0, keepdims=True)
        spot[...] = EPS * (m_ref[...] - jnp.log(total))
        for i in reversed(range(n)):
            spot_copy(i).start()
        ratio = 1.0 / total
        high = ratio.astype(jnp.bfloat16).astype(jnp.float32)
        both = jnp.where(rows == 0, high, jnp.where(rows == 1, ratio - high, 0.0)).astype(jnp.bfloat16)
        for b in range(n):
            part = dot(both, kept[:, pl.ds(b * width, width)], ((1,), (0,)))
            csum[pl.ds(b, 1), :] = jnp.sum(part, axis=0, keepdims=True)
            if (b + 1) % half == 0:
                send_sums(1, b // half)

    loads[1].wait()

    @pl.when(has_prev)
    def _():
        def prepare(y_ref, i):
            block = crossed(me, i, n)
            await_ppot(block)
            extend(y_ref, prv.at[block], ppot[block], 0.0)

        for i in order:
            @pl.when(jnp.logical_or(t > 1, i % low == 1 or low == 1))
            def _():
                landed(crossed(me, i, n), prv, prv_s, prv_r)

        reset()
        acc[...] = jnp.zeros_like(acc)
        sweep_over(prepare, prv, True)
        out_ref[...] = points[...] - STEP * (points[...] - acc[...] / l_ref[...]) + (
            math.sqrt(2.0 * STEP * TEMP) * noise[...])

    @pl.when(jnp.logical_not(has_prev))
    def _():
        out_ref[...] = points[...] + math.sqrt(2.0 * STEP * TEMP) * noise[...]

    @pl.when(has_next)
    def _():
        gam[...] = factors(1)
        side = dim + EXTRA
        lane = wide.shape[1] // 2
        y2[...] = jnp.zeros_like(y2)
        for b in range(n):
            scaled = yx[b].astype(jnp.float32) * gam[pl.ds(b, 1), :]
            high = scaled.astype(jnp.bfloat16)
            y2[b % 2, pl.ds(0, side), :] = high
            y2[b % 2, pl.ds(lane, side), :] = (scaled - high.astype(jnp.float32)).astype(jnp.bfloat16)
            part = dot(kept[:, pl.ds(b * width, width)], y2[b % 2], ((1,), (1,)))
            wide[...] = part if b == 0 else wide[...] + part
        mean = (wide[:, pl.ds(0, lane)] + wide[:, pl.ds(lane, lane)]).T
        out_ref[...] = out_ref[...] - STEP * (points[...] - mean[:dim] / mean[dim + 3:dim + 4])

    @pl.when(has_prev)
    def _():
        for i in row_order:
            to_row(nxt, nxt_s, nxt_r, i, -1).wait_send()

    @pl.when(t == 0)
    def _():
        for i in row_order:
            to_row(prv, row_s, prv_r, i, 1).wait_send()

    @pl.when(t < times - 2)
    def _():
        for i in range(n):
            to_after(i).wait_send()

    if low > 1:
        @pl.when(t == 1)
        def _():
            for i in row_order:
                to_side(prv, near_s, prv_r, crossed(me, i, n)).wait_send()

    @pl.when(has_next)
    def _():
        if low > 1:
            for i in row_order:
                to_side(nxt, side_s, nxt_r, crossed(me, i, n)).wait_send()
        for i in range(n):
            spot_copy(i).wait_send()
        for sweep in range(SWEEPS):
            for part in range(n // half):
                for i in range(1, n):
                    sum_copy(sweep, part, i, me).wait_send()


def per_device(times, n, particles, noise):
    points = particles[0]
    dim, width = points.shape
    dma = pltpu.SemaphoreType.DMA
    row = (1, width)
    tall = dim + EXTRA
    lanes = -(-tall // LANES) * LANES
    advanced = pl.pallas_call(
        functools.partial(kernel, times, n),
        out_shape=jax.ShapeDtypeStruct((dim, width), jnp.float32),
        in_specs=[pl.BlockSpec(memory_space=pl.ANY)] * 2,
        out_specs=pl.BlockSpec(memory_space=pltpu.VMEM),
        scratch_shapes=[
            pltpu.VMEM((dim, width), jnp.float32),
            pltpu.VMEM((dim, width), jnp.float32),
            pltpu.VMEM((dim, width), jnp.bfloat16),
            pltpu.VMEM((n, dim, width), jnp.bfloat16),
            pltpu.VMEM((n, dim, width), jnp.bfloat16),
            pltpu.VMEM((SWEEPS, n, n, width), jnp.float32),
            pltpu.VMEM((SWEEPS, n, width), jnp.float32),
            pltpu.VMEM((n,) + row, jnp.float32),
            pltpu.VMEM(row, jnp.float32),
            pltpu.VMEM((tall, width), jnp.bfloat16),
            pltpu.VMEM((width, tall), jnp.bfloat16),
            pltpu.VMEM((tall, width), jnp.bfloat16),
            pltpu.VMEM((tall, width), jnp.bfloat16),
            pltpu.VMEM((n, tall, width), jnp.bfloat16),
            pltpu.VMEM((2, 2 * lanes, width), jnp.bfloat16),
            pltpu.VMEM((width, n * width), jnp.bfloat16),
            pltpu.VMEM((n, width), jnp.float32),
            pltpu.VMEM((n, width), jnp.float32),
            pltpu.VMEM((2 * n, width), jnp.float32),
            pltpu.VMEM((width, width), jnp.float32),
            pltpu.VMEM((width, width), jnp.float32),
            pltpu.VMEM((width, width), jnp.bfloat16),
            pltpu.VMEM(row, jnp.float32),
            pltpu.VMEM(row, jnp.float32),
            pltpu.VMEM((dim, width), jnp.float32),
            pltpu.VMEM((width, 2 * lanes), jnp.float32),
            dma((2,)), dma((n,)), dma((n,)), dma((n,)), dma((n,)), dma((n,)), dma((n,)), dma((n,)),
            dma((SWEEPS, 2, n)), dma((SWEEPS, 2, n)), dma((n,)), dma((n,)),
        ],
        compiler_params=pltpu.CompilerParams(collective_id=0, has_side_effects=True),
    )(points, noise[0])
    return advanced[None]


def solution(mesh):
    times, n = mesh.shape["tm"], mesh.shape["dom"]
    assert n & (n - 1) == 0
    spec = P("tm", None, "dom")
    return jax.shard_map(
        functools.partial(per_device, times, n), mesh=mesh, in_specs=(spec, spec), out_specs=spec, check_vma=False)
```
